32 devices in a mesh: groups: 2 (over y), seq: 4 (over z), head: 4 (over x, core).
Axes of the slice: x: 2, y: 2, z: 4, core: 2. Of those that a mesh axis runs over, the one named last changes fastest.
Arguments:
- doc_start: int32 [1024], P(('groups', 'seq')), parts along dimension 0, may hold values from 0 to 511, as said below
- q_gdn: bfloat16 [1024, 2048], P(('groups', 'seq'), 'head'), parts along dimension 0, may hold values from -6 to 6
- k_gdn: bfloat16 [1024, 2048], P(('groups', 'seq'), 'head'), parts along dimension 0, may hold values from -6 to 6
- v_gdn: bfloat16 [1024, 4096], P(('groups', 'seq'), 'head'), parts along dimension 0, may hold values from -6 to 6
- z_gdn: bfloat16 [1024, 4096], P(('groups', 'seq'), 'head'), parts along dimension 0, may hold values from -6 to 6
- beta_logit: float32 [32, 1024], P('head', ('groups', 'seq')), parts along dimension 1, may hold values from -8 to 3
- log_decay: float32 [32, 1024], P('head', ('groups', 'seq')), parts along dimension 1, may hold values from -1 to 0
- norm_weight: float32 [128], replicated, may hold values from 0.1 to 1.9
- q_attn: bfloat16 [1024, 4096], P(('groups', 'seq'), 'head'), parts along dimension 0, may hold values from -6 to 6
- k_attn: bfloat16 [1024, 512], P(('groups', 'seq')), parts along dimension 0, may hold values from -6 to 6
- v_attn: bfloat16 [1024, 512], P(('groups', 'seq')), parts along dimension 0, may hold values from -6 to 6
- gate_attn: bfloat16 [1024, 4096], P(('groups', 'seq'), 'head'), parts along dimension 0, may hold values from -6 to 6
Outputs:
- gdn_out: bfloat16 [1024, 4096], P(('groups', 'seq'), 'head'), parts along dimension 0
- attn_out: bfloat16 [1024, 4096], P(('groups', 'seq'), 'head'), parts along dimension 0
The draws below stay inside these ranges and needn't reach their ends.
There are 2 independent parts, one for each index of `groups`. The reference program is written for one: setup_inputs(seed, part) draws one part's arguments, and reference() takes and returns one part's arrays. A program takes and returns all parts, laid end to end along the dimension named above; an argument that names none is the same for every part. Nothing has to cross between parts.
Inputs may be any that keep to these rules, and one draw needn't show every extreme that they name: Nondecreasing; doc_start[i] <= i, with equality exactly at the first token of each of the 3 documents; the first document starts at 0.
All inputs are finite; a program needn't handle non-finite values.
Results may differ from the reference program's by a relative error of at most 0.0095.
Values may be sent and summed in bfloat16 or wider, within the bound.
A program may use at most 128 MiB of HBM per device.

```python
import jax
import jax.numpy as jnp
from jax import lax

VH = 32
KH = 16
DK = 128
DV = 128
QH = 16
KVH = 2
HD_A = 256
TOK_DEV = 128
NDOCS = 3
TOKENS = 512
WINDOW = 384


def head_speed(key):
    order = jax.random.permutation(jax.random.fold_in(key, 7001), VH)
    count = VH // 2
    return order < count


def draw_log_decay(key, part):
    quick = head_speed(key)
    streams = jax.random.split(jax.random.fold_in(key, 7002), 5)
    blocks = TOKENS // TOK_DEV
    arrival_ratio = jnp.where(quick, 1.0 / 40.0, 0.4 / TOKENS)
    arrival_ratio = arrival_ratio * jax.random.uniform(streams[0], (VH,), minval=0.7, maxval=1.4)
    per_block = jnp.exp(jax.random.uniform(streams[1], (VH, blocks), minval=-0.7, maxval=0.7))
    per_token = jnp.exp(jax.random.uniform(streams[2], (VH, TOKENS), minval=-0.7, maxval=0.7))
    coarse_estimate = jnp.repeat(per_block, TOK_DEV, axis=1) * per_token
    spots = jax.random.randint(streams[3], (2,), 0, TOKENS)
    miss_count = jax.random.uniform(streams[4], (2,), minval=0.2, maxval=0.5)
    place = jnp.arange(TOKENS, dtype=jnp.int32)
    match_count = (place[None, :] == spots[:, None]).astype(jnp.float32)
    sudden_spike = jnp.sum(match_count * jnp.log(1.0 - miss_count)[:, None], axis=0)
    sluggish_level = jnp.where(quick, 0.0, 1.0)
    return -arrival_ratio[:, None] * coarse_estimate + sluggish_level[:, None] * sudden_spike[None, :]


def draw_beta_logit(key, part):
    quick = head_speed(key)
    streams = jax.random.split(jax.random.fold_in(key, 7003), 2)
    fast_level = jax.random.uniform(streams[0], (VH,), minval=0.3, maxval=0.6)
    level = jnp.where(quick, fast_level, 0.5 * DK / TOKENS)
    coarse_estimate = jnp.exp(jax.random.uniform(streams[1], (VH, TOKENS), minval=-0.7, maxval=0.7))
    beta = jnp.minimum(level[:, None] * coarse_estimate, 0.95)
    return jnp.log(beta) - jnp.log1p(-beta)


def draw_doc_start(key, part):
    order = jax.random.permutation(jax.random.fold_in(key, 7004), TOKENS - 1) + 1
    cuts = jnp.sort(order[:NDOCS - 1]).astype(jnp.int32)
    starts = jnp.concatenate([jnp.zeros((1,), jnp.int32), cuts])
    place = jnp.arange(TOKENS, dtype=jnp.int32)
    return jnp.max(jnp.where(starts[None, :] <= place[:, None], starts[None, :], 0), axis=1).astype(jnp.int32)


def draw_q_attn(key, part):
    base_key = jax.random.fold_in(key, 7006)
    width = QH * HD_A
    values = jnp.clip(jax.random.normal(base_key, (TOKENS, width)), -6.0, 6.0)
    return values.astype(jnp.bfloat16)


def draw_k_attn(key, part):
    base_key = jax.random.fold_in(key, 7007)
    width = KVH * HD_A
    values = jnp.clip(jax.random.normal(base_key, (TOKENS, width)), -6.0, 6.0)
    return values.astype(jnp.bfloat16)


def levels(rng, dims, cuts, least, high):
    def one(axis_at, shards_of):
        heights = jax.random.uniform(jax.random.fold_in(jax.random.fold_in(rng, 6), axis_at), (shards_of,), jnp.float32, least / len(cuts), high / len(cuts))
        return jnp.repeat(jnp.exp(heights), dims[axis_at] // shards_of).reshape((-1,) + (1,) * (len(dims) - axis_at - 1))

    loudness = one(*cuts[0])
    for cut in cuts[1:]:
        loudness = loudness * one(*cut)
    return loudness


def normal_values(rng, extent, spread, most, cuts=(), held_as=jnp.bfloat16):
    drawn = jax.random.normal(rng, extent, jnp.float32) * spread
    if len(cuts) > 0:
        drawn = levels(rng, extent, cuts, -0.22, 0.18) * drawn
    return jnp.clip(drawn, min=-most, max=most).astype(held_as)


def setup_inputs(seed: int = 0, part: int = 0) -> dict:
    key_list = jax.random.split(jax.random.key(seed), 13)
    part_splits = jax.random.split(jax.random.fold_in(key_list[12], part), 13)
    return {
        "doc_start": draw_doc_start(jax.random.fold_in(jax.random.fold_in(key_list[12], part), 71), part),
        "q_gdn": normal_values(part_splits[1], (TOKENS, KH * DK), 1.0, 6.0, ((0, 4), (1, 4))),
        "k_gdn": normal_values(part_splits[2], (TOKENS, KH * DK), 1.0, 6.0, ((0, 4), (1, 4))),
        "v_gdn": normal_values(part_splits[3], (TOKENS, VH * DV), 1.0, 6.0, ((0, 4), (1, 4))),
        "z_gdn": normal_values(part_splits[4], (TOKENS, VH * DV), 1.0, 6.0, ((0, 4), (1, 4))),
        "beta_logit": draw_beta_logit(jax.random.fold_in(jax.random.fold_in(key_list[12], part), 71), part),
        "log_decay": draw_log_decay(jax.random.fold_in(jax.random.fold_in(key_list[12], part), 71), part),
        "norm_weight": jnp.clip(1.0 + 0.18 * jax.random.normal(key_list[7], (DV,), jnp.float32), 0.1, 1.9),
        "q_attn": draw_q_attn(jax.random.fold_in(jax.random.fold_in(key_list[12], part), 71), part),
        "k_attn": draw_k_attn(jax.random.fold_in(jax.random.fold_in(key_list[12], part), 71), part),
        "v_attn": normal_values(part_splits[10], (TOKENS, KVH * HD_A), 1.0, 6.0, ((0, 4),)),
        "gate_attn": normal_values(part_splits[11], (TOKENS, QH * HD_A), 1.0, 6.0, ((0, 4), (1, 4))),
    }


HIGH = lax.Precision.HIGHEST

def unit_rows(values):
    return values * lax.rsqrt(lax.optimization_barrier(jnp.sum(values * values, axis=-1, keepdims=True)) + 1e-06)

def delta_rule(doc_start, q_gdn, k_gdn, v_gdn, beta_logit, log_decay):
    length = q_gdn.shape[0]
    repeat = VH // KH
    query = jnp.repeat(unit_rows(q_gdn.astype(jnp.float32).reshape(length, KH, DK)), repeat, axis=1)
    keys = jnp.repeat(unit_rows(k_gdn.astype(jnp.float32).reshape(length, KH, DK)), repeat, axis=1)
    values = v_gdn.astype(jnp.float32).reshape(length, VH, DV)
    beta = jax.nn.sigmoid(beta_logit).T
    decay = jnp.exp(log_decay).T
    place = jnp.arange(length, dtype=jnp.int32)
    carry_on = (doc_start != place).astype(jnp.float32)

    def advance(state, inputs):
        query_t, key_t, value_t, beta_t, decay_t, carry_t = inputs
        state = state * (decay_t * carry_t)[:, None, None]
        guess = jnp.einsum('hvk,hk->hv', state, key_t, precision=HIGH)
        update = beta_t[:, None] * (value_t - guess)
        state = state + update[:, :, None] * key_t[:, None, :]
        return (state, jnp.einsum('hvk,hk->hv', state, query_t, precision=HIGH))
    anchor = jnp.zeros((VH, DV, DK), jnp.float32)
    _, mixed = lax.scan(advance, anchor, (query, keys, values, beta, decay, carry_on))
    return mixed

def gated_norm(mixed, z_gdn, norm_weight):
    length = mixed.shape[0]
    gate = z_gdn.astype(jnp.float32).reshape(length, VH, DV)
    factor = lax.rsqrt(lax.optimization_barrier(jnp.mean(mixed * mixed, axis=-1, keepdims=True)) + 1e-06)
    normed = mixed * factor * norm_weight * jax.nn.silu(gate)
    return normed.reshape(length, VH * DV).astype(jnp.bfloat16)

def window_attention(doc_start, q_attn, k_attn, v_attn, gate_attn):
    length = q_attn.shape[0]
    span = min(WINDOW + TOK_DEV, length)
    group = QH // KVH
    factor = HD_A ** (-0.5)

    def one_block(index):
        q_start = (index * TOK_DEV).astype(jnp.int32)
        k_start = jnp.clip(q_start - WINDOW, 0, length - span).astype(jnp.int32)
        query = lax.dynamic_slice_in_dim(q_attn, q_start, TOK_DEV, 0).astype(jnp.float32).reshape(TOK_DEV, QH, HD_A)
        gate = lax.dynamic_slice_in_dim(gate_attn, q_start, TOK_DEV, 0).astype(jnp.float32).reshape(TOK_DEV, QH, HD_A)
        docs = lax.dynamic_slice_in_dim(doc_start, q_start, TOK_DEV, 0)
        keys = lax.dynamic_slice_in_dim(k_attn, k_start, span, 0).astype(jnp.float32).reshape(span, KVH, HD_A)
        values = lax.dynamic_slice_in_dim(v_attn, k_start, span, 0).astype(jnp.float32).reshape(span, KVH, HD_A)
        keys = jnp.repeat(keys, group, axis=1)
        values = jnp.repeat(values, group, axis=1)
        scores = jnp.einsum('qhd,khd->hqk', query, keys, precision=HIGH) * factor
        q_place = q_start + jnp.arange(TOK_DEV, dtype=jnp.int32)
        k_place = k_start + jnp.arange(span, dtype=jnp.int32)
        lower = jnp.maximum(docs, q_place - WINDOW + 1)
        visible = (k_place[None, :] >= lower[:, None]) & (k_place[None, :] <= q_place[:, None])
        masked = jnp.where(visible[None], scores, -jnp.inf)
        peak = lax.optimization_barrier(jnp.max(masked, axis=-1, keepdims=True))
        weights = jnp.exp(masked - peak)
        total = lax.optimization_barrier(jnp.sum(weights, axis=-1))
        rounded = lax.optimization_barrier(weights.astype(jnp.bfloat16)).astype(jnp.float32)
        mixed = jnp.einsum('hqk,khd->qhd', rounded, values, precision=HIGH)
        result = mixed / total.T[:, :, None] * jax.nn.sigmoid(gate)
        return result.reshape(TOK_DEV, QH * HD_A).astype(jnp.bfloat16)
    blocks = lax.map(one_block, jnp.arange(length // TOK_DEV, dtype=jnp.int32))
    return blocks.reshape(length, QH * HD_A)

def reference(doc_start, q_gdn, k_gdn, v_gdn, z_gdn, beta_logit, log_decay, norm_weight, q_attn, k_attn, v_attn, gate_attn):
    mixed = delta_rule(doc_start, q_gdn, k_gdn, v_gdn, beta_logit, log_decay)
    gdn_out = gated_norm(mixed, z_gdn, norm_weight)
    attn_out = window_attention(doc_start, q_attn, k_attn, v_attn, gate_attn)
    return (gdn_out, attn_out)
```

```python
import functools

import jax
import jax.numpy as jnp
from jax import lax
from jax.experimental import pallas as pl
from jax.experimental.pallas import tpu as pltpu
from jax.sharding import PartitionSpec as P

DK = 128
DV = 128
QH = 16
KVH = 2
HD_A = 256
NEG = -1e30

MESH = pl.DeviceIdType.MESH
BF = jnp.bfloat16
F32 = jnp.float32


def dot(a, b):
    return jnp.dot(a.astype(BF), b.astype(BF), preferred_element_type=F32)


def dot_t(a, b):
    return lax.dot_general(a, b, (((1,), (1,)), ((), ())), preferred_element_type=F32)


def unit_rows(values):
    return values * lax.rsqrt(jnp.sum(values * values, axis=-1, keepdims=True) + 1e-06)


def running_sum(rows, lane):
    width = rows.shape[1]
    step = 1
    while step < width:
        rows = rows + jnp.where(lane >= step, pltpu.roll(rows, step, 1), 0.0)
        step *= 2
    return rows


def kernel(
    devices,
    seen,
    doc_ref,
    q_ref,
    k_ref,
    v_ref,
    z_ref,
    beta_ref,
    gate_ref,
    norm_ref,
    qa_ref,
    ka_ref,
    va_ref,
    ga_ref,
    gdn_ref,
    attn_ref,
    keys_buf,
    vals_buf,
    state_in,
    state_out,
    local_buf,
    reach_buf,
    map_buf,
    add_buf,
    kv_send,
    kv_recv,
    st_send,
    st_recv,
):
    me = lax.axis_index("seq")
    length = q_ref.shape[0]
    heads = v_ref.shape[1] // DV
    key_heads = q_ref.shape[1] // DK
    repeat = heads // key_heads
    attn_heads = qa_ref.shape[1] // HD_A
    kv = lax.axis_index("head") * attn_heads // (QH // KVH)
    columns = pl.ds(pl.multiple_of(kv * HD_A, HD_A), HD_A)
    anchor = me * length

    barrier = pltpu.get_barrier_semaphore()
    for r in range(1, seen + 1):
        @pl.when(me + r < devices)
        def _():
            pl.semaphore_signal(barrier, inc=1, device_id={"seq": me + r}, device_id_type=MESH)

        @pl.when(me - r >= 0)
        def _():
            pl.semaphore_signal(barrier, inc=1, device_id={"seq": me - r}, device_id_type=MESH)

    pl.semaphore_wait(barrier, jnp.minimum(me, seen) + jnp.minimum(devices - 1 - me, seen))

    def kv_copies(r):
        rows = pl.ds((seen - r) * length, length)
        return [
            pltpu.make_async_remote_copy(
                src_ref=src.at[:, columns],
                dst_ref=dst.at[rows, :],
                send_sem=kv_send.at[r - 1, which],
                recv_sem=kv_recv.at[r - 1, which],
                device_id={"seq": me + r},
                device_id_type=MESH,
            )
            for which, (src, dst) in enumerate(((ka_ref, keys_buf), (va_ref, vals_buf)))
        ]

    def state_copy(h):
        return pltpu.make_async_remote_copy(
            src_ref=state_out.at[h],
            dst_ref=state_in.at[h],
            send_sem=st_send.at[h],
            recv_sem=st_recv.at[h],
            device_id={"seq": me + 1},
            device_id_type=MESH,
        )

    for r in range(1, seen + 1):
        @pl.when(me + r < devices)
        def _():
            for copy in kv_copies(r):
                copy.start()

    row = lax.broadcasted_iota(jnp.int32, (length, length), 0)
    col = lax.broadcasted_iota(jnp.int32, (length, length), 1)
    lane = lax.broadcasted_iota(jnp.int32, (heads, length), 1)
    docs = doc_ref[...]
    run = running_sum(gate_ref[...], lane)
    beta = jax.nn.sigmoid(beta_ref[...])
    alive = docs < anchor
    entry = jnp.where(alive, jnp.exp(run), 0.0)
    last_run = run[:, length - 1 :]
    doc_last = docs[:, length - 1 :]
    tail = jnp.where(doc_last <= anchor + lane, jnp.exp(last_run - run), 0.0)
    entry_last = entry[:, length - 1 :]
    doc_rows = jnp.broadcast_to((docs - anchor).astype(F32), (heads, length))
    stacked = jnp.concatenate([run, beta, entry, doc_rows], axis=0)
    stacked = jnp.concatenate(
        [stacked, jnp.zeros((length - stacked.shape[0], length), F32)], axis=0
    )
    cols = stacked.T

    def column(kind, h):
        at = kind * heads + h
        return cols[:, at : at + 1]

    doc_col = column(3, 0).astype(jnp.int32)
    same = (col <= row) & (doc_col <= col)
    strict = same & (col < row)
    eye = jnp.where(row == col, 1.0, 0.0).astype(F32)
    differ = row ^ col
    levels = 0
    while (1 << levels) < length:
        levels += 1

    def local(group):
        qn, kn, knt, gram, cross = {}, {}, {}, {}, {}
        for g in sorted({h // repeat for h in group}):
            at = slice(g * DK, (g + 1) * DK)
            qn[g] = unit_rows(q_ref[:, at].astype(F32))
            kn[g] = unit_rows(k_ref[:, at].astype(F32))
            knt[g] = kn[g].T
            both = dot(jnp.concatenate([kn[g], qn[g]], axis=0), knt[g])
            gram[g], cross[g] = both[:length], both[length:]
        lower, scores, inverse = {}, {}, {}
        for h in group:
            g = h // repeat
            spread = jnp.where(same, column(0, h) - run[h : h + 1, :], 0.0)
            decay = jnp.where(same, jnp.exp(spread), 0.0)
            lower[h] = jnp.where(strict, column(1, h) * decay * gram[g], 0.0)
            scores[h] = (cross[g] * decay).astype(BF)
            inverse[h] = eye - jnp.where(differ == 1, lower[h], 0.0)
        for level in range(1, levels):
            mask = (differ >> level) == 1
            half = {}
            for h in group:
                part = jnp.where(mask, lower[h], 0.0)
                half[h] = dot(inverse[h], part)
            for h in group:
                inverse[h] = inverse[h] - dot(half[h], inverse[h])
        for h in group:
            g = h // repeat
            values = v_ref[:, h * DV : (h + 1) * DV].astype(F32)
            b = column(1, h)
            right = jnp.concatenate([b * values, (b * column(2, h)) * kn[g]], axis=1)
            solved = dot(inverse[h], right)
            tail_keys = knt[g] * tail[h : h + 1, :]
            left = jnp.concatenate([scores[h], tail_keys.astype(BF)], axis=0)
            made = dot(left, solved)
            local_buf[h] = made[:length, :DV]
            reach_buf[h] = (column(2, h) * qn[g] - made[:length, DV:]).astype(BF)
            map_buf[h] = (entry_last[h : h + 1, :] * eye - made[length:, DV:]).astype(BF)
            add_buf[h] = made[length:, :DV]

            @pl.when(me == 0)
            def _():
                state_in[h] = jnp.zeros(state_in.shape[1:], BF)
                state_out[h] = add_buf[h].astype(BF)
                if devices > 1:
                    state_copy(h).start()

    per_group = 4
    for first in range(0, heads, per_group):
        local(list(range(first, min(first + per_group, heads))))

    for h in range(heads):
        @pl.when(me > 0)
        def _():
            state_copy(h).wait_recv()

            @pl.when(me < devices - 1)
            def _():
                fresh = add_buf[h] + dot(map_buf[h], state_in[h])
                state_out[h] = fresh.astype(BF)
                state_copy(h).start()

    own = pl.ds(seen * length, length)
    keys_buf[own, :] = ka_ref[:, columns]
    vals_buf[own, :] = va_ref[:, columns]
    for r in range(1, seen + 1):
        @pl.when(me - r >= 0)
        def _():
            for copy in kv_copies(r):
                copy.wait_recv()

        @pl.when(me - r < 0)
        def _():
            rows = pl.ds((seen - r) * length, length)
            keys_buf[rows, :] = jnp.zeros((length, HD_A), BF)
            vals_buf[rows, :] = jnp.zeros((length, HD_A), BF)

    span = (seen + 1) * length
    window = (devices // 2 + 1) * length
    q_at = lax.broadcasted_iota(jnp.int32, (length, span), 0)
    k_at = lax.broadcasted_iota(jnp.int32, (length, span), 1) - seen * length
    floor = jnp.maximum(doc_col, q_at - window + 1)
    visible = (k_at >= floor) & (k_at <= q_at)
    factor = HD_A ** (-0.5)
    for a in range(attn_heads):
        at = slice(a * HD_A, (a + 1) * HD_A)
        raw = dot_t(qa_ref[:, at], keys_buf[...]) * factor
        masked = jnp.where(visible, raw, NEG)
        peak = jnp.max(masked, axis=-1, keepdims=True)
        weights = jnp.exp(masked - peak)
        total = jnp.sum(weights, axis=-1, keepdims=True)
        mixed = jnp.dot(weights.astype(BF), vals_buf[...], preferred_element_type=F32)
        gated = mixed / total * jax.nn.sigmoid(ga_ref[:, at].astype(F32))
        attn_ref[:, at] = gated.astype(BF)

    gain = norm_ref[...]
    for h in range(heads):
        at = slice(h * DV, (h + 1) * DV)
        mixed = local_buf[h] + dot(reach_buf[h], state_in[h])
        spread = lax.rsqrt(jnp.mean(mixed * mixed, axis=-1, keepdims=True) + 1e-06)
        gate = z_ref[:, at].astype(F32)
        gdn_ref[:, at] = (mixed * spread * gain * jax.nn.silu(gate)).astype(BF)

    for r in range(1, seen + 1):
        @pl.when(me + r < devices)
        def _():
            for copy in kv_copies(r):
                copy.wait_send()

    if devices > 1:
        @pl.when(me < devices - 1)
        def _():
            for h in range(heads):
                state_copy(h).wait_send()


def shards(
    devices,
    doc_start,
    q_gdn,
    k_gdn,
    v_gdn,
    z_gdn,
    beta_logit,
    log_decay,
    norm_weight,
    q_attn,
    k_attn,
    v_attn,
    gate_attn,
):
    length = q_gdn.shape[0]
    heads = v_gdn.shape[1] // DV
    seen = min(devices // 2 + 1, devices - 1)
    span = (seen + 1) * length
    whole = pl.BlockSpec(memory_space=pltpu.VMEM)
    return pl.pallas_call(
        functools.partial(kernel, devices, seen),
        out_shape=(
            jax.ShapeDtypeStruct(v_gdn.shape, BF),
            jax.ShapeDtypeStruct(q_attn.shape, BF),
        ),
        in_specs=[whole] * 12,
        out_specs=(whole, whole),
        scratch_shapes=[
            pltpu.VMEM((span, HD_A), BF),
            pltpu.VMEM((span, HD_A), BF),
            pltpu.VMEM((heads, DK, DV), BF),
            pltpu.VMEM((heads, DK, DV), BF),
            pltpu.VMEM((heads, length, DV), F32),
            pltpu.VMEM((heads, length, DK), BF),
            pltpu.VMEM((heads, DK, DK), BF),
            pltpu.VMEM((heads, DK, DV), F32),
            pltpu.SemaphoreType.DMA((seen, 2)),
            pltpu.SemaphoreType.DMA((seen, 2)),
            pltpu.SemaphoreType.DMA((heads,)),
            pltpu.SemaphoreType.DMA((heads,)),
        ],
        compiler_params=pltpu.CompilerParams(collective_id=0, has_side_effects=True),
    )(
        doc_start.reshape(1, length),
        q_gdn,
        k_gdn,
        v_gdn,
        z_gdn,
        beta_logit,
        log_decay,
        norm_weight.reshape(1, DV),
        q_attn,
        k_attn,
        v_attn,
        gate_attn,
    )


def solution(mesh):
    return jax.shard_map(
        functools.partial(shards, mesh.shape["seq"]),
        mesh=mesh,
        in_specs=(
            P(("groups", "seq")),
            P(("groups", "seq"), "head"),
            P(("groups", "seq"), "head"),
            P(("groups", "seq"), "head"),
            P(("groups", "seq"), "head"),
            P("head", ("groups", "seq")),
            P("head", ("groups", "seq")),
            P(),
            P(("groups", "seq"), "head"),
            P(("groups", "seq"), None),
            P(("groups", "seq"), None),
            P(("groups", "seq"), "head"),
        ),
        out_specs=(P(("groups", "seq"), "head"), P(("groups", "seq"), "head")),
        check_vma=False,
    )
```

```python
import functools

import jax
import jax.numpy as jnp
from jax import lax
from jax.experimental import pallas as pl
from jax.experimental.pallas import tpu as pltpu
from jax.sharding import PartitionSpec as P

DK = 128
DV = 128
QH = 16
KVH = 2
HD_A = 256
NEG = -1e30

MESH = pl.DeviceIdType.MESH
BF = jnp.bfloat16
F32 = jnp.float32


def dot(a, b):
    return jnp.dot(a.astype(BF), b.astype(BF), preferred_element_type=F32)


def dot_t(a, b):
    return lax.dot_general(a, b, (((1,), (1,)), ((), ())), preferred_element_type=F32)


def running_sum(rows, lane):
    width = rows.shape[1]
    step = 1
    while step < width:
        rows = rows + jnp.where(lane >= step, pltpu.roll(rows, step, 1), 0.0)
        step *= 2
    return rows


def kernel(
    devices,
    seen,
    doc_ref,
    q_ref,
    k_ref,
    v_ref,
    z_ref,
    beta_ref,
    gate_ref,
    norm_ref,
    qa_ref,
    ka_ref,
    va_ref,
    ga_ref,
    gdn_ref,
    attn_ref,
    keys_buf,
    vals_buf,
    state_in,
    state_out,
    local_buf,
    reach_buf,
    map_buf,
    add_buf,
    qn_buf,
    score_buf,
    solved_buf,
    kv_send,
    kv_recv,
    st_send,
    st_recv,
):
    me = lax.axis_index("seq")
    length = q_ref.shape[0]
    heads = v_ref.shape[1] // DV
    key_heads = q_ref.shape[1] // DK
    repeat = heads // key_heads
    attn_heads = qa_ref.shape[1] // HD_A
    kv = lax.axis_index("head") * attn_heads // (QH // KVH)
    columns = pl.ds(pl.multiple_of(kv * HD_A, HD_A), HD_A)
    anchor = me * length

    barrier = pltpu.get_barrier_semaphore()
    for r in range(1, seen + 1):
        @pl.when(me + r < devices)
        def _():
            pl.semaphore_signal(barrier, inc=1, device_id={"seq": me + r}, device_id_type=MESH)

        @pl.when(me - r >= 0)
        def _():
            pl.semaphore_signal(barrier, inc=1, device_id={"seq": me - r}, device_id_type=MESH)

    pl.semaphore_wait(barrier, jnp.minimum(me, seen) + jnp.minimum(devices - 1 - me, seen))

    def kv_copies(r):
        rows = pl.ds((seen - r) * length, length)
        return [
            pltpu.make_async_remote_copy(
                src_ref=src.at[:, columns],
                dst_ref=dst.at[rows, :],
                send_sem=kv_send.at[r - 1, which],
                recv_sem=kv_recv.at[r - 1, which],
                device_id={"seq": me + r},
                device_id_type=MESH,
            )
            for which, (src, dst) in enumerate(((ka_ref, keys_buf), (va_ref, vals_buf)))
        ]

    def state_copy(h):
        return pltpu.make_async_remote_copy(
            src_ref=state_out.at[h],
            dst_ref=state_in.at[h],
            send_sem=st_send.at[h],
            recv_sem=st_recv.at[h],
            device_id={"seq": me + 1},
            device_id_type=MESH,
        )

    for r in range(1, seen + 1):
        @pl.when(me + r < devices)
        def _():
            for copy in kv_copies(r):
                copy.start()

    row = lax.broadcasted_iota(jnp.int32, (length, length), 0)
    col = lax.broadcasted_iota(jnp.int32, (length, length), 1)
    lane = lax.broadcasted_iota(jnp.int32, (heads, length), 1)
    docs = doc_ref[...]
    run = running_sum(gate_ref[...], lane)
    beta = jax.nn.sigmoid(beta_ref[...])
    alive = docs < anchor
    entry = jnp.where(alive, jnp.exp(run), 0.0)
    last_run = run[:, length - 1 :]
    doc_last = docs[:, length - 1 :]
    tail = jnp.where(doc_last <= anchor + lane, jnp.exp(last_run - run), 0.0)
    entry_last = entry[:, length - 1 :]
    doc_rows = jnp.broadcast_to((docs - anchor).astype(F32), (heads, length))
    stacked = jnp.concatenate([run, beta, entry, doc_rows], axis=0)
    stacked = jnp.concatenate(
        [stacked, jnp.zeros((length - stacked.shape[0], length), F32)], axis=0
    )
    cols = stacked.T

    def column(kind, h):
        at = kind * heads + h
        return cols[:, at : at + 1]

    doc_col = column(3, 0).astype(jnp.int32)
    same = (col <= row) & (doc_col <= col)
    strict = same & (col < row)
    eye = jnp.where(row == col, 1.0, 0.0).astype(F32)
    differ = row ^ col
    levels = 0
    while (1 << levels) < length:
        levels += 1

    ones = jnp.ones((DK, DK), BF)

    def square_sum(values):
        squares = values * values
        high = squares.astype(BF)
        low = (squares - high.astype(F32)).astype(BF)
        return jnp.dot(high, ones, preferred_element_type=F32) + jnp.dot(
            low, ones, preferred_element_type=F32
        )

    def unit_rows(values):
        return values * lax.rsqrt(square_sum(values) + 1e-06)

    def state_part(group):
        kn, knt, gram, cross = {}, {}, {}, {}
        for g in sorted({h // repeat for h in group}):
            at = slice(g * DK, (g + 1) * DK)
            qn = unit_rows(q_ref[:, at].astype(F32)).astype(BF)
            kn[g] = unit_rows(k_ref[:, at].astype(F32)).astype(BF)
            qn_buf[g] = qn
            knt[g] = kn[g].T
            both = dot(jnp.concatenate([kn[g], qn], axis=0), knt[g])
            gram[g], cross[g] = both[:length], both[length:]
        inverse = {}
        for h in group:
            g = h // repeat
            spread = jnp.where(same, column(0, h) - run[h : h + 1, :], 0.0)
            decay = jnp.where(same, jnp.exp(spread), 0.0)
            lower = jnp.where(strict, column(1, h) * decay * gram[g], 0.0)
            score_buf[h] = (cross[g] * decay).astype(BF)
            inverse[h] = eye + lower
        for level in range(levels):
            mask = (differ >> level) == 1
            for h in group:
                whole = inverse[h]
                part = jnp.where(mask, whole, 0.0)
                inverse[h] = jnp.where(mask, 0.0, whole) - dot(part, whole)
        solved = {}
        for h in group:
            g = h // repeat
            values = v_ref[:, h * DV : (h + 1) * DV].astype(F32)
            b = column(1, h)
            right = jnp.concatenate(
                [b * values, (b * column(2, h)) * kn[g].astype(F32)], axis=1
            )
            solved[h] = dot(inverse[h], right).astype(BF)
            solved_buf[h] = solved[h]
        for h in group:
            g = h // repeat
            tail_keys = (knt[g].astype(F32) * tail[h : h + 1, :]).astype(BF)
            made = dot(tail_keys, solved[h])
            map_buf[h] = (entry_last[h : h + 1, :] * eye - made[:, DV:]).astype(BF)
            add_buf[h] = made[:, :DV]
            state_out[h] = made[:, :DV].astype(BF)

        if devices > 1:
            @pl.when(me == 0)
            def _():
                for h in group:
                    state_copy(h).start()

    per_group = 4
    for first in range(0, heads, per_group):
        state_part(list(range(first, min(first + per_group, heads))))

    def relay():
        for h in range(heads):
            state_copy(h).wait_recv()

            @pl.when(me < devices - 1)
            def _():
                fresh = add_buf[h] + dot(map_buf[h], state_in[h])
                state_out[h] = fresh.astype(BF)
                state_copy(h).start()

    @pl.when(me == 0)
    def _():
        state_in[...] = jnp.zeros(state_in.shape, BF)

    @pl.when(me == 1)
    def _():
        relay()

    own = pl.ds(seen * length, length)
    keys_buf[own, :] = ka_ref[:, columns]
    vals_buf[own, :] = va_ref[:, columns]
    for h in range(heads):
        made = dot(score_buf[h], solved_buf[h])
        local_buf[h] = made[:, :DV]
        through = column(2, h) * qn_buf[h // repeat].astype(F32)
        reach_buf[h] = (through - made[:, DV:]).astype(BF)

    if devices > 2:
        @pl.when(me == 2)
        def _():
            relay()

    for r in range(1, seen + 1):
        @pl.when(me - r >= 0)
        def _():
            for copy in kv_copies(r):
                copy.wait_recv()

        @pl.when(me - r < 0)
        def _():
            rows = pl.ds((seen - r) * length, length)
            keys_buf[rows, :] = jnp.zeros((length, HD_A), BF)
            vals_buf[rows, :] = jnp.zeros((length, HD_A), BF)

    span = (seen + 1) * length
    window = (devices // 2 + 1) * length
    q_at = lax.broadcasted_iota(jnp.int32, (length, span), 0)
    k_at = lax.broadcasted_iota(jnp.int32, (length, span), 1) - seen * length
    floor = jnp.maximum(doc_col, q_at - window + 1)
    visible = (k_at >= floor) & (k_at <= q_at)
    factor = HD_A ** (-0.5)
    for a in range(attn_heads):
        at = slice(a * HD_A, (a + 1) * HD_A)
        raw = dot_t(qa_ref[:, at], keys_buf[...]) * factor
        masked = jnp.where(visible, raw, NEG)
        peak = jnp.max(masked, axis=-1, keepdims=True)
        weights = jnp.exp(masked - peak)
        total = jnp.sum(weights, axis=-1, keepdims=True)
        mixed = jnp.dot(weights.astype(BF), vals_buf[...], preferred_element_type=F32)
        gated = mixed / total * jax.nn.sigmoid(ga_ref[:, at].astype(F32))
        attn_ref[:, at] = gated.astype(BF)

    if devices > 3:
        @pl.when(me >= 3)
        def _():
            relay()

    gain = norm_ref[...]
    for h in range(heads):
        at = slice(h * DV, (h + 1) * DV)
        mixed = local_buf[h] + dot(reach_buf[h], state_in[h])
        spread = lax.rsqrt(square_sum(mixed) * (1.0 / DV) + 1e-06)
        gate = z_ref[:, at].astype(F32)
        gdn_ref[:, at] = (mixed * spread * gain * jax.nn.silu(gate)).astype(BF)

    for r in range(1, seen + 1):
        @pl.when(me + r < devices)
        def _():
            for copy in kv_copies(r):
                copy.wait_send()

    if devices > 1:
        @pl.when(me < devices - 1)
        def _():
            for h in range(heads):
                state_copy(h).wait_send()


def shards(
    devices,
    doc_start,
    q_gdn,
    k_gdn,
    v_gdn,
    z_gdn,
    beta_logit,
    log_decay,
    norm_weight,
    q_attn,
    k_attn,
    v_attn,
    gate_attn,
):
    length = q_gdn.shape[0]
    heads = v_gdn.shape[1] // DV
    seen = min(devices // 2 + 1, devices - 1)
    span = (seen + 1) * length
    whole = pl.BlockSpec(memory_space=pltpu.VMEM)
    return pl.pallas_call(
        functools.partial(kernel, devices, seen),
        out_shape=(
            jax.ShapeDtypeStruct(v_gdn.shape, BF),
            jax.ShapeDtypeStruct(q_attn.shape, BF),
        ),
        in_specs=[whole] * 12,
        out_specs=(whole, whole),
        scratch_shapes=[
            pltpu.VMEM((span, HD_A), BF),
            pltpu.VMEM((span, HD_A), BF),
            pltpu.VMEM((heads, DK, DV), BF),
            pltpu.VMEM((heads, DK, DV), BF),
            pltpu.VMEM((heads, length, DV), F32),
            pltpu.VMEM((heads, length, DK), BF),
            pltpu.VMEM((heads, DK, DK), BF),
            pltpu.VMEM((heads, DK, DV), F32),
            pltpu.VMEM((q_gdn.shape[1] // DK, length, DK), BF),
            pltpu.VMEM((heads, length, length), BF),
            pltpu.VMEM((heads, length, DV + DK), BF),
            pltpu.SemaphoreType.DMA((seen, 2)),
            pltpu.SemaphoreType.DMA((seen, 2)),
            pltpu.SemaphoreType.DMA((heads,)),
            pltpu.SemaphoreType.DMA((heads,)),
        ],
        compiler_params=pltpu.CompilerParams(collective_id=0, has_side_effects=True),
    )(
        doc_start.reshape(1, length),
        q_gdn,
        k_gdn,
        v_gdn,
        z_gdn,
        beta_logit,
        log_decay,
        norm_weight.reshape(1, DV),
        q_attn,
        k_attn,
        v_attn,
        gate_attn,
    )


def solution(mesh):
    return jax.shard_map(
        functools.partial(shards, mesh.shape["seq"]),
        mesh=mesh,
        in_specs=(
            P(("groups", "seq")),
            P(("groups", "seq"), "head"),
            P(("groups", "seq"), "head"),
            P(("groups", "seq"), "head"),
            P(("groups", "seq"), "head"),
            P("head", ("groups", "seq")),
            P("head", ("groups", "seq")),
            P(),
            P(("groups", "seq"), "head"),
            P(("groups", "seq"), None),
            P(("groups", "seq"), None),
            P(("groups", "seq"), "head"),
        ),
        out_specs=(P(("groups", "seq"), "head"), P(("groups", "seq"), "head")),
        check_vma=False,
    )
```

```python
import functools

import jax
import jax.numpy as jnp
from jax import lax
from jax.experimental import pallas as pl
from jax.experimental.pallas import tpu as pltpu
from jax.sharding import PartitionSpec as P

DK = 128
DV = 128
QH = 16
KVH = 2
HD_A = 256
NEG = -1e30

MESH = pl.DeviceIdType.MESH
BF = jnp.bfloat16
F32 = jnp.float32


def dot(a, b):
    return jnp.dot(a.astype(BF), b.astype(BF), preferred_element_type=F32)


def dot_t(a, b):
    return lax.dot_general(a, b, (((1,), (1,)), ((), ())), preferred_element_type=F32)


def running_sum(rows, lane):
    width = rows.shape[1]
    step = 1
    while step < width:
        rows = rows + jnp.where(lane >= step, pltpu.roll(rows, step, 1), 0.0)
        step *= 2
    return rows


def kernel(
    devices,
    seen,
    doc_ref,
    q_ref,
    k_ref,
    v_ref,
    z_ref,
    beta_ref,
    gate_ref,
    norm_ref,
    qa_ref,
    ka_ref,
    va_ref,
    ga_ref,
    gdn_ref,
    attn_ref,
    kv_buf,
    state_in,
    state_out,
    local_buf,
    reach_buf,
    map_buf,
    add_buf,
    qn_buf,
    score_buf,
    solved_buf,
    kv_send,
    kv_recv,
    ex_send,
    ex_recv,
    st_send,
    st_recv,
):
    me = lax.axis_index("seq")
    length = q_ref.shape[0]
    heads = v_ref.shape[1] // DV
    key_heads = q_ref.shape[1] // DK
    repeat = heads // key_heads
    attn_heads = qa_ref.shape[1] // HD_A
    kv = lax.axis_index("head") * attn_heads // (QH // KVH)
    columns = pl.ds(pl.multiple_of(kv * HD_A, HD_A), HD_A)
    anchor = me * length

    head = lax.axis_index("head")
    part = head % 2
    partner = head + 1 - 2 * part

    barrier = pltpu.get_barrier_semaphore()
    pl.semaphore_signal(barrier, inc=1, device_id={"head": partner}, device_id_type=MESH)

    @pl.when(me < devices - 1)
    def _():
        pl.semaphore_signal(barrier, inc=1, device_id={"seq": me + 1}, device_id_type=MESH)

    @pl.when(me > 0)
    def _():
        pl.semaphore_signal(barrier, inc=1, device_id={"seq": me - 1}, device_id_type=MESH)

    pl.semaphore_wait(barrier, 1 + jnp.minimum(me, 1) + jnp.minimum(devices - 1 - me, 1))

    def rows_of(r):
        return pl.ds((seen - r) * length, length)

    def hop(r, source):
        return pltpu.make_async_remote_copy(
            src_ref=source,
            dst_ref=kv_buf.at[part, rows_of(r), :],
            send_sem=kv_send.at[r - 1],
            recv_sem=kv_recv.at[r - 1],
            device_id={"seq": me + 1},
            device_id_type=MESH,
        )

    def exchange(r):
        return pltpu.make_async_remote_copy(
            src_ref=kv_buf.at[part, rows_of(r), :],
            dst_ref=kv_buf.at[part, rows_of(r), :],
            send_sem=ex_send.at[r - 1],
            recv_sem=ex_recv.at[r - 1],
            device_id={"head": partner},
            device_id_type=MESH,
        )

    def held(r):
        return kv_buf.at[part, rows_of(r), :]

    def forward(r):
        @pl.when(me >= r)
        def _():
            hop(r, held(r)).wait_recv()
            exchange(r).start()
            if r < seen:
                @pl.when(me < devices - 1)
                def _():
                    hop(r + 1, held(r)).start()

    def state_copy(h):
        return pltpu.make_async_remote_copy(
            src_ref=state_out.at[h],
            dst_ref=state_in.at[h],
            send_sem=st_send.at[h],
            recv_sem=st_recv.at[h],
            device_id={"seq": me + 1},
            device_id_type=MESH,
        )

    @pl.when(me < devices - 1)
    def _():
        for which, source in enumerate((ka_ref, va_ref)):
            @pl.when(part == which)
            def _():
                hop(1, source.at[:, columns]).start()

    row = lax.broadcasted_iota(jnp.int32, (length, length), 0)
    col = lax.broadcasted_iota(jnp.int32, (length, length), 1)
    lane = lax.broadcasted_iota(jnp.int32, (heads, length), 1)
    docs = doc_ref[...]
    run = running_sum(gate_ref[...], lane)
    beta = jax.nn.sigmoid(beta_ref[...])
    alive = docs < anchor
    entry = jnp.where(alive, jnp.exp(run), 0.0)
    last_run = run[:, length - 1 :]
    doc_last = docs[:, length - 1 :]
    tail = jnp.where(doc_last <= anchor + lane, jnp.exp(last_run - run), 0.0)
    entry_last = entry[:, length - 1 :]
    doc_rows = jnp.broadcast_to((docs - anchor).astype(F32), (heads, length))
    stacked = jnp.concatenate([run, beta, entry, doc_rows], axis=0)
    stacked = jnp.concatenate(
        [stacked, jnp.zeros((length - stacked.shape[0], length), F32)], axis=0
    )
    cols = stacked.T

    def column(kind, h):
        at = kind * heads + h
        return cols[:, at : at + 1]

    doc_col = column(3, 0).astype(jnp.int32)
    same = (col <= row) & (doc_col <= col)
    strict = same & (col < row)
    eye = jnp.where(row == col, 1.0, 0.0).astype(F32)
    differ = row ^ col
    levels = 0
    while (1 << levels) < length:
        levels += 1

    ones = jnp.ones((DK, DK), BF)

    def square_sum(values):
        squares = values * values
        high = squares.astype(BF)
        low = (squares - high.astype(F32)).astype(BF)
        return jnp.dot(high, ones, preferred_element_type=F32) + jnp.dot(
            low, ones, preferred_element_type=F32
        )

    def unit_rows(values):
        return values * lax.rsqrt(square_sum(values) + 1e-06)

    def state_part(group):
        kn, knt, gram, cross = {}, {}, {}, {}
        for g in sorted({h // repeat for h in group}):
            at = slice(g * DK, (g + 1) * DK)
            qn = unit_rows(q_ref[:, at].astype(F32)).astype(BF)
            kn[g] = unit_rows(k_ref[:, at].astype(F32)).astype(BF)
            qn_buf[g] = qn
            knt[g] = kn[g].T
            both = dot(jnp.concatenate([kn[g], qn], axis=0), knt[g])
            gram[g], cross[g] = both[:length], both[length:]
        inverse = {}
        for h in group:
            g = h // repeat
            spread = jnp.where(same, column(0, h) - run[h : h + 1, :], 0.0)
            decay = jnp.where(same, jnp.exp(spread), 0.0)
            lower = jnp.where(strict, column(1, h) * decay * gram[g], 0.0)
            score_buf[h] = (cross[g] * decay).astype(BF)
            inverse[h] = eye + lower
        for level in range(levels):
            mask = (differ >> level) == 1
            for h in group:
                whole = inverse[h]
                part = jnp.where(mask, whole, 0.0)
                inverse[h] = jnp.where(mask, 0.0, whole) - dot(part, whole)
        solved = {}
        for h in group:
            g = h // repeat
            values = v_ref[:, h * DV : (h + 1) * DV].astype(F32)
            b = column(1, h)
            right = jnp.concatenate(
                [b * values, (b * column(2, h)) * kn[g].astype(F32)], axis=1
            )
            solved[h] = dot(inverse[h], right).astype(BF)
            solved_buf[h] = solved[h]
        for h in group:
            g = h // repeat
            tail_keys = (knt[g].astype(F32) * tail[h : h + 1, :]).astype(BF)
            made = dot(tail_keys, solved[h])
            map_buf[h] = (entry_last[h : h + 1, :] * eye - made[:, DV:]).astype(BF)
            add_buf[h] = made[:, :DV]
            state_out[h] = made[:, :DV].astype(BF)

        if devices > 1:
            @pl.when(me == 0)
            def _():
                for h in group:
                    state_copy(h).start()

    per_group = 4
    ahead = 0
    for first in range(0, heads, per_group):
        state_part(list(range(first, min(first + per_group, heads))))
        if ahead < seen:
            ahead += 1
            forward(ahead)

    def relay():
        for h in range(heads):
            state_copy(h).wait_recv()

            @pl.when(me < devices - 1)
            def _():
                fresh = add_buf[h] + dot(map_buf[h], state_in[h])
                state_out[h] = fresh.astype(BF)
                state_copy(h).start()

    @pl.when(me == 0)
    def _():
        state_in[...] = jnp.zeros(state_in.shape, BF)

    @pl.when(me == 1)
    def _():
        relay()

    own = pl.ds(seen * length, length)
    kv_buf[0, own, :] = ka_ref[:, columns]
    kv_buf[1, own, :] = va_ref[:, columns]
    for h in range(heads):
        made = dot(score_buf[h], solved_buf[h])
        local_buf[h] = made[:, :DV]
        through = column(2, h) * qn_buf[h // repeat].astype(F32)
        reach_buf[h] = (through - made[:, DV:]).astype(BF)

    if devices > 2:
        @pl.when(me == 2)
        def _():
            relay()

    for r in range(ahead + 1, seen + 1):
        forward(r)
    for r in range(1, seen + 1):
        @pl.when(me >= r)
        def _():
            exchange(r).wait_recv()

        @pl.when(me < r)
        def _():
            kv_buf[:, rows_of(r), :] = jnp.zeros((2, length, HD_A), BF)

    span = (seen + 1) * length
    window = (devices // 2 + 1) * length
    q_at = lax.broadcasted_iota(jnp.int32, (length, span), 0)
    k_at = lax.broadcasted_iota(jnp.int32, (length, span), 1) - seen * length
    floor = jnp.maximum(doc_col, q_at - window + 1)
    visible = (k_at >= floor) & (k_at <= q_at)
    factor = HD_A ** (-0.5)
    for a in range(attn_heads):
        at = slice(a * HD_A, (a + 1) * HD_A)
        raw = dot_t(qa_ref[:, at], kv_buf[0]) * factor
        masked = jnp.where(visible, raw, NEG)
        peak = jnp.max(masked, axis=-1, keepdims=True)
        weights = jnp.exp(masked - peak)
        total = jnp.sum(weights, axis=-1, keepdims=True)
        mixed = jnp.dot(weights.astype(BF), kv_buf[1], preferred_element_type=F32)
        gated = mixed / total * jax.nn.sigmoid(ga_ref[:, at].astype(F32))
        attn_ref[:, at] = gated.astype(BF)

    if devices > 3:
        @pl.when(me >= 3)
        def _():
            relay()

    gain = norm_ref[...]
    for h in range(heads):
        at = slice(h * DV, (h + 1) * DV)
        mixed = local_buf[h] + dot(reach_buf[h], state_in[h])
        spread = lax.rsqrt(square_sum(mixed) * (1.0 / DV) + 1e-06)
        gate = z_ref[:, at].astype(F32)
        gdn_ref[:, at] = (mixed * spread * gain * jax.nn.silu(gate)).astype(BF)

    @pl.when(me < devices - 1)
    def _():
        hop(1, held(1)).wait_send()

    for r in range(1, seen + 1):
        @pl.when(me >= r)
        def _():
            exchange(r).wait_send()
            if r < seen:
                @pl.when(me < devices - 1)
                def _():
                    hop(r + 1, held(r)).wait_send()

    if devices > 1:
        @pl.when(me < devices - 1)
        def _():
            for h in range(heads):
                state_copy(h).wait_send()


def shards(
    devices,
    doc_start,
    q_gdn,
    k_gdn,
    v_gdn,
    z_gdn,
    beta_logit,
    log_decay,
    norm_weight,
    q_attn,
    k_attn,
    v_attn,
    gate_attn,
):
    length = q_gdn.shape[0]
    heads = v_gdn.shape[1] // DV
    seen = min(devices // 2 + 1, devices - 1)
    span = (seen + 1) * length
    whole = pl.BlockSpec(memory_space=pltpu.VMEM)
    return pl.pallas_call(
        functools.partial(kernel, devices, seen),
        out_shape=(
            jax.ShapeDtypeStruct(v_gdn.shape, BF),
            jax.ShapeDtypeStruct(q_attn.shape, BF),
        ),
        in_specs=[whole] * 12,
        out_specs=(whole, whole),
        scratch_shapes=[
            pltpu.VMEM((2, span, HD_A), BF),
            pltpu.VMEM((heads, DK, DV), BF),
            pltpu.VMEM((heads, DK, DV), BF),
            pltpu.VMEM((heads, length, DV), F32),
            pltpu.VMEM((heads, length, DK), BF),
            pltpu.VMEM((heads, DK, DK), BF),
            pltpu.VMEM((heads, DK, DV), F32),
            pltpu.VMEM((q_gdn.shape[1] // DK, length, DK), BF),
            pltpu.VMEM((heads, length, length), BF),
            pltpu.VMEM((heads, length, DV + DK), BF),
            pltpu.SemaphoreType.DMA((seen,)),
            pltpu.SemaphoreType.DMA((seen,)),
            pltpu.SemaphoreType.DMA((seen,)),
            pltpu.SemaphoreType.DMA((seen,)),
            pltpu.SemaphoreType.DMA((heads,)),
            pltpu.SemaphoreType.DMA((heads,)),
        ],
        compiler_params=pltpu.CompilerParams(collective_id=0, has_side_effects=True),
    )(
        doc_start.reshape(1, length),
        q_gdn,
        k_gdn,
        v_gdn,
        z_gdn,
        beta_logit,
        log_decay,
        norm_weight.reshape(1, DV),
        q_attn,
        k_attn,
        v_attn,
        gate_attn,
    )


def solution(mesh):
    return jax.shard_map(
        functools.partial(shards, mesh.shape["seq"]),
        mesh=mesh,
        in_specs=(
            P(("groups", "seq")),
            P(("groups", "seq"), "head"),
            P(("groups", "seq"), "head"),
            P(("groups", "seq"), "head"),
            P(("groups", "seq"), "head"),
            P("head", ("groups", "seq")),
            P("head", ("groups", "seq")),
            P(),
            P(("groups", "seq"), "head"),
            P(("groups", "seq"), None),
            P(("groups", "seq"), None),
            P(("groups", "seq"), "head"),
        ),
        out_specs=(P(("groups", "seq"), "head"), P(("groups", "seq"), "head")),
        check_vma=False,
    )
```

```python
import functools

import jax
import jax.numpy as jnp
from jax import lax
from jax.experimental import pallas as pl
from jax.experimental.pallas import tpu as pltpu
from jax.sharding import PartitionSpec as P

DK = 128
DV = 128
QH = 16
KVH = 2
HD_A = 256
NEG = -1e30

MESH = pl.DeviceIdType.MESH
BF = jnp.bfloat16
F32 = jnp.float32


def dot(a, b):
    return jnp.dot(a.astype(BF), b.astype(BF), preferred_element_type=F32)


def dot_t(a, b):
    return lax.dot_general(a, b, (((1,), (1,)), ((), ())), preferred_element_type=F32)


def running_sum(rows, lane):
    width = rows.shape[1]
    step = 1
    while step < width:
        rows = rows + jnp.where(lane >= step, pltpu.roll(rows, step, 1), 0.0)
        step *= 2
    return rows


def kernel(
    devices,
    seen,
    doc_ref,
    q_ref,
    k_ref,
    v_ref,
    z_ref,
    beta_ref,
    gate_ref,
    norm_ref,
    qa_ref,
    ka_ref,
    va_ref,
    ga_ref,
    gdn_ref,
    attn_ref,
    kv_buf,
    state_in,
    state_out,
    local_buf,
    reach_buf,
    map_buf,
    add_buf,
    kn_buf,
    knt_buf,
    decay_buf,
    solved_buf,
    kv_send,
    kv_recv,
    ex_send,
    ex_recv,
    st_send,
    st_recv,
):
    me = lax.axis_index("seq")
    length = q_ref.shape[0]
    heads = v_ref.shape[1] // DV
    key_heads = q_ref.shape[1] // DK
    repeat = heads // key_heads
    attn_heads = qa_ref.shape[1] // HD_A
    kv = lax.axis_index("head") * attn_heads // (QH // KVH)
    columns = pl.ds(pl.multiple_of(kv * HD_A, HD_A), HD_A)
    anchor = me * length

    head = lax.axis_index("head")
    part = head % 2
    partner = head + 1 - 2 * part

    barrier = pltpu.get_barrier_semaphore()
    pl.semaphore_signal(barrier, inc=1, device_id={"head": partner}, device_id_type=MESH)

    @pl.when(me < devices - 1)
    def _():
        pl.semaphore_signal(barrier, inc=1, device_id={"seq": me + 1}, device_id_type=MESH)

    @pl.when(me > 0)
    def _():
        pl.semaphore_signal(barrier, inc=1, device_id={"seq": me - 1}, device_id_type=MESH)

    pl.semaphore_wait(barrier, 1 + jnp.minimum(me, 1) + jnp.minimum(devices - 1 - me, 1))

    def rows_of(r):
        return pl.ds((seen - r) * length, length)

    def hop(r, source):
        return pltpu.make_async_remote_copy(
            src_ref=source,
            dst_ref=kv_buf.at[part, rows_of(r), :],
            send_sem=kv_send.at[r - 1],
            recv_sem=kv_recv.at[r - 1],
            device_id={"seq": me + 1},
            device_id_type=MESH,
        )

    def exchange(r):
        return pltpu.make_async_remote_copy(
            src_ref=kv_buf.at[part, rows_of(r), :],
            dst_ref=kv_buf.at[part, rows_of(r), :],
            send_sem=ex_send.at[r - 1],
            recv_sem=ex_recv.at[r - 1],
            device_id={"head": partner},
            device_id_type=MESH,
        )

    def held(r):
        return kv_buf.at[part, rows_of(r), :]

    def forward(r):
        @pl.when(me >= r)
        def _():
            hop(r, held(r)).wait_recv()
            exchange(r).start()
            if r < seen:
                @pl.when(me < devices - 1)
                def _():
                    hop(r + 1, held(r)).start()

    def state_copy(h):
        return pltpu.make_async_remote_copy(
            src_ref=state_out.at[h],
            dst_ref=state_in.at[h],
            send_sem=st_send.at[h],
            recv_sem=st_recv.at[h],
            device_id={"seq": me + 1},
            device_id_type=MESH,
        )

    @pl.when(me < devices - 1)
    def _():
        for which, source in enumerate((ka_ref, va_ref)):
            @pl.when(part == which)
            def _():
                hop(1, source.at[:, columns]).start()

    row = lax.broadcasted_iota(jnp.int32, (length, length), 0)
    col = lax.broadcasted_iota(jnp.int32, (length, length), 1)
    lane = lax.broadcasted_iota(jnp.int32, (heads, length), 1)
    docs = doc_ref[...]
    run = running_sum(gate_ref[...], lane)
    beta = jax.nn.sigmoid(beta_ref[...])
    alive = docs < anchor
    entry = jnp.where(alive, jnp.exp(run), 0.0)
    last_run = run[:, length - 1 :]
    doc_last = docs[:, length - 1 :]
    tail = jnp.where(doc_last <= anchor + lane, jnp.exp(last_run - run), 0.0)
    entry_last = entry[:, length - 1 :]
    doc_rows = jnp.broadcast_to((docs - anchor).astype(F32), (heads, length))
    stacked = jnp.concatenate([run, beta, entry, doc_rows], axis=0)
    stacked = jnp.concatenate(
        [stacked, jnp.zeros((length - stacked.shape[0], length), F32)], axis=0
    )
    cols = stacked.T

    def column(kind, h):
        at = kind * heads + h
        return cols[:, at : at + 1]

    doc_col = column(3, 0).astype(jnp.int32)
    same = (col <= row) & (doc_col <= col)
    strict = same & (col < row)
    eye = jnp.where(row == col, 1.0, 0.0).astype(F32)
    differ = row ^ col
    levels = 0
    while (1 << levels) < length:
        levels += 1

    ones = jnp.ones((DK, DK), BF)

    def square_sum(values):
        squares = values * values
        high = squares.astype(BF)
        low = (squares - high.astype(F32)).astype(BF)
        return jnp.dot(high, ones, preferred_element_type=F32) + jnp.dot(
            low, ones, preferred_element_type=F32
        )

    def unit_rows(values):
        return values * lax.rsqrt(square_sum(values) + 1e-06)

    gram, knt, lower = {}, {}, {}

    def key_part(g):
        kn = unit_rows(k_ref[:, g * DK : (g + 1) * DK].astype(F32)).astype(BF)
        knt[g] = kn.T
        kn_buf[g] = kn
        knt_buf[g] = knt[g]
        gram[g] = dot(kn, knt[g])

    def gate_part(h):
        spread = jnp.where(same, column(0, h) - run[h : h + 1, :], 0.0)
        decay = jnp.where(same, jnp.exp(spread), 0.0)
        decay_buf[h] = decay
        lower[h] = jnp.where(strict, column(1, h) * decay * gram[h // repeat], 0.0)

    def preparations(group):
        todo = []
        for h in group:
            if h // repeat not in gram:
                gram[h // repeat] = None
                todo.append(functools.partial(key_part, h // repeat))
            todo.append(functools.partial(gate_part, h))
        return todo

    def state_part(group, beside):
        beside = list(beside)
        inverse = {h: eye + lower[h] for h in group}
        for level in range(levels):
            mask = (differ >> level) == 1
            for h in group:
                whole = inverse[h]
                part = jnp.where(mask, whole, 0.0)
                inverse[h] = jnp.where(mask, 0.0, whole) - dot(part, whole)
            if beside:
                beside.pop(0)()
        for task in beside:
            task()
        for h in group:
            g = h // repeat
            values = v_ref[:, h * DV : (h + 1) * DV].astype(F32)
            b = column(1, h)
            right = jnp.concatenate(
                [b * values, (b * column(2, h)) * kn_buf[g].astype(F32)], axis=1
            )
            solved = dot(inverse[h], right).astype(BF)
            solved_buf[h] = solved
            tail_keys = (knt_buf[g].astype(F32) * tail[h : h + 1, :]).astype(BF)
            made = dot(tail_keys, solved)
            map_buf[h] = (entry_last[h : h + 1, :] * eye - made[:, DV:]).astype(BF)
            add_buf[h] = made[:, :DV]
            state_out[h] = made[:, :DV].astype(BF)

        if devices > 1:
            @pl.when(me == 0)
            def _():
                for h in group:
                    state_copy(h).start()

    per_group = 4
    groups = [
        list(range(first, min(first + per_group, heads))) for first in range(0, heads, per_group)
    ]
    for task in preparations(groups[0]):
        task()
    ahead = 0
    for at, group in enumerate(groups):
        state_part(group, preparations(groups[at + 1]) if at + 1 < len(groups) else ())
        if ahead < seen:
            ahead += 1
            forward(ahead)

    def relay():
        for h in range(heads):
            state_copy(h).wait_recv()

            @pl.when(me < devices - 1)
            def _():
                fresh = add_buf[h] + dot(map_buf[h], state_in[h])
                state_out[h] = fresh.astype(BF)
                state_copy(h).start()

    @pl.when(me == 0)
    def _():
        state_in[...] = jnp.zeros(state_in.shape, BF)

    @pl.when(me == 1)
    def _():
        relay()

    own = pl.ds(seen * length, length)
    kv_buf[0, own, :] = ka_ref[:, columns]
    kv_buf[1, own, :] = va_ref[:, columns]
    for g in range(key_heads):
        qn = unit_rows(q_ref[:, g * DK : (g + 1) * DK].astype(F32)).astype(BF)
        cross = dot(qn, knt_buf[g])
        for h in range(g * repeat, (g + 1) * repeat):
            made = dot(cross * decay_buf[h], solved_buf[h])
            local_buf[h] = made[:, :DV]
            reach_buf[h] = (column(2, h) * qn.astype(F32) - made[:, DV:]).astype(BF)

    if devices > 2:
        @pl.when(me == 2)
        def _():
            relay()

    for r in range(ahead + 1, seen + 1):
        forward(r)
    for r in range(1, seen + 1):
        @pl.when(me >= r)
        def _():
            exchange(r).wait_recv()

        @pl.when(me < r)
        def _():
            kv_buf[:, rows_of(r), :] = jnp.zeros((2, length, HD_A), BF)

    span = (seen + 1) * length
    window = (devices // 2 + 1) * length
    q_at = lax.broadcasted_iota(jnp.int32, (length, span), 0)
    k_at = lax.broadcasted_iota(jnp.int32, (length, span), 1) - seen * length
    floor = jnp.maximum(doc_col, q_at - window + 1)
    visible = (k_at >= floor) & (k_at <= q_at)
    factor = HD_A ** (-0.5)
    for a in range(attn_heads):
        at = slice(a * HD_A, (a + 1) * HD_A)
        raw = dot_t(qa_ref[:, at], kv_buf[0]) * factor
        masked = jnp.where(visible, raw, NEG)
        peak = jnp.max(masked, axis=-1, keepdims=True)
        weights = jnp.exp(masked - peak)
        total = jnp.sum(weights, axis=-1, keepdims=True)
        mixed = jnp.dot(weights.astype(BF), kv_buf[1], preferred_element_type=F32)
        gated = mixed / total * jax.nn.sigmoid(ga_ref[:, at].astype(F32))
        attn_ref[:, at] = gated.astype(BF)

    if devices > 3:
        @pl.when(me >= 3)
        def _():
            relay()

    gain = norm_ref[...]
    for h in range(heads):
        at = slice(h * DV, (h + 1) * DV)
        mixed = local_buf[h] + dot(reach_buf[h], state_in[h])
        spread = lax.rsqrt(square_sum(mixed) * (1.0 / DV) + 1e-06)
        gate = z_ref[:, at].astype(F32)
        gdn_ref[:, at] = (mixed * spread * gain * jax.nn.silu(gate)).astype(BF)

    @pl.when(me < devices - 1)
    def _():
        hop(1, held(1)).wait_send()

    for r in range(1, seen + 1):
        @pl.when(me >= r)
        def _():
            exchange(r).wait_send()
            if r < seen:
                @pl.when(me < devices - 1)
                def _():
                    hop(r + 1, held(r)).wait_send()

    if devices > 1:
        @pl.when(me < devices - 1)
        def _():
            for h in range(heads):
                state_copy(h).wait_send()


def shards(
    devices,
    doc_start,
    q_gdn,
    k_gdn,
    v_gdn,
    z_gdn,
    beta_logit,
    log_decay,
    norm_weight,
    q_attn,
    k_attn,
    v_attn,
    gate_attn,
):
    length = q_gdn.shape[0]
    heads = v_gdn.shape[1] // DV
    seen = min(devices // 2 + 1, devices - 1)
    span = (seen + 1) * length
    whole = pl.BlockSpec(memory_space=pltpu.VMEM)
    return pl.pallas_call(
        functools.partial(kernel, devices, seen),
        out_shape=(
            pltpu.VMEM(v_gdn.shape, BF),
            pltpu.VMEM(q_attn.shape, BF),
        ),
        in_specs=[whole] * 12,
        out_specs=(whole, whole),
        scratch_shapes=[
            pltpu.VMEM((2, span, HD_A), BF),
            pltpu.VMEM((heads, DK, DV), BF),
            pltpu.VMEM((heads, DK, DV), BF),
            pltpu.VMEM((heads, length, DV), F32),
            pltpu.VMEM((heads, length, DK), BF),
            pltpu.VMEM((heads, DK, DK), BF),
            pltpu.VMEM((heads, DK, DV), F32),
            pltpu.VMEM((q_gdn.shape[1] // DK, length, DK), BF),
            pltpu.VMEM((q_gdn.shape[1] // DK, DK, length), BF),
            pltpu.VMEM((heads, length, length), F32),
            pltpu.VMEM((heads, length, DV + DK), BF),
            pltpu.SemaphoreType.DMA((seen,)),
            pltpu.SemaphoreType.DMA((seen,)),
            pltpu.SemaphoreType.DMA((seen,)),
            pltpu.SemaphoreType.DMA((seen,)),
            pltpu.SemaphoreType.DMA((heads,)),
            pltpu.SemaphoreType.DMA((heads,)),
        ],
        compiler_params=pltpu.CompilerParams(collective_id=0, has_side_effects=True),
    )(
        doc_start.reshape(1, length),
        q_gdn,
        k_gdn,
        v_gdn,
        z_gdn,
        beta_logit,
        log_decay,
        norm_weight.reshape(1, DV),
        q_attn,
        k_attn,
        v_attn,
        gate_attn,
    )


def solution(mesh):
    return jax.shard_map(
        functools.partial(shards, mesh.shape["seq"]),
        mesh=mesh,
        in_specs=(
            P(("groups", "seq")),
            P(("groups", "seq"), "head"),
            P(("groups", "seq"), "head"),
            P(("groups", "seq"), "head"),
            P(("groups", "seq"), "head"),
            P("head", ("groups", "seq")),
            P("head", ("groups", "seq")),
            P(),
            P(("groups", "seq"), "head"),
            P(("groups", "seq"), None),
            P(("groups", "seq"), None),
            P(("groups", "seq"), "head"),
        ),
        out_specs=(P(("groups", "seq"), "head"), P(("groups", "seq"), "head")),
        check_vma=False,
    )
```

```python
import functools

import jax
import jax.numpy as jnp
from jax import lax
from jax.experimental import pallas as pl
from jax.experimental.pallas import tpu as pltpu
from jax.sharding import PartitionSpec as P

DK = 128
DV = 128
QH = 16
KVH = 2
HD_A = 256
NEG = -1e30

MESH = pl.DeviceIdType.MESH
BF = jnp.bfloat16
F32 = jnp.float32


def dot(a, b):
    return jnp.dot(a.astype(BF), b.astype(BF), preferred_element_type=F32)


def dot_t(a, b):
    return lax.dot_general(a, b, (((1,), (1,)), ((), ())), preferred_element_type=F32)


def running_sum(rows, lane):
    width = rows.shape[1]
    step = 1
    while step < width:
        rows = rows + jnp.where(lane >= step, pltpu.roll(rows, step, 1), 0.0)
        step *= 2
    return rows


def kernel(
    devices,
    seen,
    doc_ref,
    q_ref,
    k_ref,
    v_ref,
    z_ref,
    beta_ref,
    gate_ref,
    norm_ref,
    qa_ref,
    ka_ref,
    va_ref,
    ga_ref,
    gdn_ref,
    attn_ref,
    kv_buf,
    state_in,
    state_out,
    local_buf,
    reach_buf,
    map_buf,
    add_buf,
    kn_buf,
    knt_buf,
    decay_buf,
    solved_buf,
    kv_send,
    kv_recv,
    ex_send,
    ex_recv,
    st_send,
    st_recv,
):
    me = lax.axis_index("seq")
    length = q_ref.shape[0]
    heads = v_ref.shape[1] // DV
    key_heads = q_ref.shape[1] // DK
    repeat = heads // key_heads
    attn_heads = qa_ref.shape[1] // HD_A
    kv = lax.axis_index("head") * attn_heads // (QH // KVH)
    columns = pl.ds(pl.multiple_of(kv * HD_A, HD_A), HD_A)
    anchor = me * length

    head = lax.axis_index("head")
    part = head % 2
    partner = head + 1 - 2 * part

    barrier = pltpu.get_barrier_semaphore()
    pl.semaphore_signal(barrier, inc=1, device_id={"head": partner}, device_id_type=MESH)

    @pl.when(me < devices - 1)
    def _():
        pl.semaphore_signal(barrier, inc=1, device_id={"seq": me + 1}, device_id_type=MESH)

    @pl.when(me > 0)
    def _():
        pl.semaphore_signal(barrier, inc=1, device_id={"seq": me - 1}, device_id_type=MESH)

    pl.semaphore_wait(barrier, 1 + jnp.minimum(me, 1) + jnp.minimum(devices - 1 - me, 1))

    def rows_of(r):
        return pl.ds((seen - r) * length, length)

    def hop(r, source):
        return pltpu.make_async_remote_copy(
            src_ref=source,
            dst_ref=kv_buf.at[part, rows_of(r), :],
            send_sem=kv_send.at[r - 1],
            recv_sem=kv_recv.at[r - 1],
            device_id={"seq": me + 1},
            device_id_type=MESH,
        )

    def exchange(r):
        return pltpu.make_async_remote_copy(
            src_ref=kv_buf.at[part, rows_of(r), :],
            dst_ref=kv_buf.at[part, rows_of(r), :],
            send_sem=ex_send.at[r - 1],
            recv_sem=ex_recv.at[r - 1],
            device_id={"head": partner},
            device_id_type=MESH,
        )

    def held(r):
        return kv_buf.at[part, rows_of(r), :]

    def forward(r):
        @pl.when(me >= r)
        def _():
            hop(r, held(r)).wait_recv()
            exchange(r).start()
            if r < seen:
                @pl.when(me < devices - 1)
                def _():
                    hop(r + 1, held(r)).start()

    def state_copy(h):
        return pltpu.make_async_remote_copy(
            src_ref=state_out.at[h],
            dst_ref=state_in.at[h],
            send_sem=st_send.at[h],
            recv_sem=st_recv.at[h],
            device_id={"seq": me + 1},
            device_id_type=MESH,
        )

    @pl.when(me < devices - 1)
    def _():
        for which, source in enumerate((ka_ref, va_ref)):
            @pl.when(part == which)
            def _():
                hop(1, source.at[:, columns]).start()

    row = lax.broadcasted_iota(jnp.int32, (length, length), 0)
    col = lax.broadcasted_iota(jnp.int32, (length, length), 1)
    lane = lax.broadcasted_iota(jnp.int32, (heads, length), 1)
    docs = doc_ref[...]
    run = running_sum(gate_ref[...], lane)
    beta = jax.nn.sigmoid(beta_ref[...])
    alive = docs < anchor
    entry = jnp.where(alive, jnp.exp(run), 0.0)
    last_run = run[:, length - 1 :]
    doc_last = docs[:, length - 1 :]
    tail = jnp.where(doc_last <= anchor + lane, jnp.exp(last_run - run), 0.0)
    entry_last = entry[:, length - 1 :]
    doc_rows = jnp.broadcast_to((docs - anchor).astype(F32), (heads, length))
    stacked = jnp.concatenate([run, beta, entry, doc_rows], axis=0)
    stacked = jnp.concatenate(
        [stacked, jnp.zeros((length - stacked.shape[0], length), F32)], axis=0
    )
    cols = stacked.T

    def column(kind, h):
        at = kind * heads + h
        return cols[:, at : at + 1]

    doc_col = column(3, 0).astype(jnp.int32)
    same = (col <= row) & (doc_col <= col)
    strict = same & (col < row)
    eye = jnp.where(row == col, 1.0, 0.0).astype(F32)
    differ = row ^ col
    levels = 0
    while (1 << levels) < length:
        levels += 1

    ones = jnp.ones((DK, DK), BF)

    def square_sum(values):
        squares = values * values
        high = squares.astype(BF)
        low = (squares - high.astype(F32)).astype(BF)
        return jnp.dot(high, ones, preferred_element_type=F32) + jnp.dot(
            low, ones, preferred_element_type=F32
        )

    def unit_rows(values):
        return values * lax.rsqrt(square_sum(values) + 1e-06)

    gram, knt, lower = {}, {}, {}

    def key_part(g):
        kn = unit_rows(k_ref[:, g * DK : (g + 1) * DK].astype(F32)).astype(BF)
        knt[g] = kn.T
        kn_buf[g] = kn
        knt_buf[g] = knt[g]
        gram[g] = dot(kn, knt[g])

    def gate_part(h):
        spread = jnp.where(same, column(0, h) - run[h : h + 1, :], 0.0)
        decay = jnp.where(same, jnp.exp(spread), 0.0)
        decay_buf[h] = decay
        lower[h] = jnp.where(strict, column(1, h) * decay * gram[h // repeat], 0.0)

    def preparations(group):
        todo = []
        for h in group:
            if h // repeat not in gram:
                gram[h // repeat] = None
                todo.append(functools.partial(key_part, h // repeat))
            todo.append(functools.partial(gate_part, h))
        return todo

    def state_part(group, beside):
        beside = list(beside)
        inverse = {h: eye + lower[h] for h in group}
        for level in range(levels):
            mask = (differ >> level) == 1
            for h in group:
                whole = inverse[h]
                part = jnp.where(mask, whole, 0.0)
                inverse[h] = jnp.where(mask, 0.0, whole) - dot(part, whole)
            if beside:
                beside.pop(0)()
        for task in beside:
            task()
        for h in group:
            g = h // repeat
            values = v_ref[:, h * DV : (h + 1) * DV].astype(F32)
            b = column(1, h)
            right = jnp.concatenate(
                [b * values, (b * column(2, h)) * kn_buf[g].astype(F32)], axis=1
            )
            solved = dot(inverse[h], right).astype(BF)
            solved_buf[h] = solved
            tail_keys = (knt_buf[g].astype(F32) * tail[h : h + 1, :]).astype(BF)
            made = dot(tail_keys, solved)
            map_buf[h] = (entry_last[h : h + 1, :] * eye - made[:, DV:]).astype(BF)
            add_buf[h] = made[:, :DV]
            state_out[h] = made[:, :DV].astype(BF)

        if devices > 1:
            @pl.when(me == 0)
            def _():
                for h in group:
                    state_copy(h).start()

    per_group = 2
    groups = [
        list(range(first, min(first + per_group, heads))) for first in range(0, heads, per_group)
    ]
    for task in preparations(groups[0]):
        task()
    ahead = 0
    for at, group in enumerate(groups):
        state_part(group, preparations(groups[at + 1]) if at + 1 < len(groups) else ())
        if at % 2 == 1 and ahead < seen:
            ahead += 1
            forward(ahead)

    def relay(chosen):
        for h in chosen:
            state_copy(h).wait_recv()

            @pl.when(me < devices - 1)
            def _():
                fresh = add_buf[h] + dot(map_buf[h], state_in[h])
                state_out[h] = fresh.astype(BF)
                state_copy(h).start()

    @pl.when(me == 0)
    def _():
        state_in[...] = jnp.zeros(state_in.shape, BF)

    @pl.when(me == 1)
    def _():
        relay(range(heads))

    own = pl.ds(seen * length, length)
    kv_buf[0, own, :] = ka_ref[:, columns]
    kv_buf[1, own, :] = va_ref[:, columns]
    for g in range(key_heads):
        qn = unit_rows(q_ref[:, g * DK : (g + 1) * DK].astype(F32)).astype(BF)
        cross = dot(qn, knt_buf[g])
        for h in range(g * repeat, (g + 1) * repeat):
            made = dot(cross * decay_buf[h], solved_buf[h])
            local_buf[h] = made[:, :DV]
            reach_buf[h] = (column(2, h) * qn.astype(F32) - made[:, DV:]).astype(BF)

    if devices > 2:
        @pl.when(me == 2)
        def _():
            relay(range(heads))

    for r in range(ahead + 1, seen + 1):
        forward(r)
    for r in range(1, seen + 1):
        @pl.when(me >= r)
        def _():
            exchange(r).wait_recv()

        @pl.when(me < r)
        def _():
            kv_buf[:, rows_of(r), :] = jnp.zeros((2, length, HD_A), BF)

    span = (seen + 1) * length
    window = (devices // 2 + 1) * length
    q_at = lax.broadcasted_iota(jnp.int32, (length, span), 0)
    k_at = lax.broadcasted_iota(jnp.int32, (length, span), 1) - seen * length
    floor = jnp.maximum(doc_col, q_at - window + 1)
    visible = (k_at >= floor) & (k_at <= q_at)
    factor = HD_A ** (-0.5)
    for a in range(attn_heads):
        at = slice(a * HD_A, (a + 1) * HD_A)
        raw = dot_t(qa_ref[:, at], kv_buf[0]) * factor
        masked = jnp.where(visible, raw, NEG)
        peak = jnp.max(masked, axis=-1, keepdims=True)
        weights = jnp.exp(masked - peak)
        total = jnp.sum(weights, axis=-1, keepdims=True)
        mixed = jnp.dot(weights.astype(BF), kv_buf[1], preferred_element_type=F32)
        gated = mixed / total * jax.nn.sigmoid(ga_ref[:, at].astype(F32))
        attn_ref[:, at] = gated.astype(BF)

    gain = norm_ref[...]
    for first in range(0, heads, per_group):
        chosen = range(first, min(first + per_group, heads))
        if devices > 3:
            @pl.when(me >= 3)
            def _():
                relay(chosen)

        for h in chosen:
            at = slice(h * DV, (h + 1) * DV)
            mixed = local_buf[h] + dot(reach_buf[h], state_in[h])
            spread = lax.rsqrt(square_sum(mixed) * (1.0 / DV) + 1e-06)
            gate = z_ref[:, at].astype(F32)
            gdn_ref[:, at] = (mixed * spread * gain * jax.nn.silu(gate)).astype(BF)

    @pl.when(me < devices - 1)
    def _():
        hop(1, held(1)).wait_send()

    for r in range(1, seen + 1):
        @pl.when(me >= r)
        def _():
            exchange(r).wait_send()
            if r < seen:
                @pl.when(me < devices - 1)
                def _():
                    hop(r + 1, held(r)).wait_send()

    if devices > 1:
        @pl.when(me < devices - 1)
        def _():
            for h in range(heads):
                state_copy(h).wait_send()


def store(first_ref, second_ref, first_out, second_out, sems):
    copies = [
        pltpu.make_async_copy(first_ref, first_out, sems.at[0]),
        pltpu.make_async_copy(second_ref, second_out, sems.at[1]),
    ]
    for copy in copies:
        copy.start()
    for copy in copies:
        copy.wait()


def shards(
    devices,
    doc_start,
    q_gdn,
    k_gdn,
    v_gdn,
    z_gdn,
    beta_logit,
    log_decay,
    norm_weight,
    q_attn,
    k_attn,
    v_attn,
    gate_attn,
):
    length = q_gdn.shape[0]
    heads = v_gdn.shape[1] // DV
    seen = min(devices // 2 + 1, devices - 1)
    span = (seen + 1) * length
    whole = pl.BlockSpec(memory_space=pltpu.VMEM)
    mixed = pl.pallas_call(
        functools.partial(kernel, devices, seen),
        out_shape=(
            pltpu.VMEM(v_gdn.shape, BF),
            pltpu.VMEM(q_attn.shape, BF),
        ),
        in_specs=[whole] * 12,
        out_specs=(whole, whole),
        scratch_shapes=[
            pltpu.VMEM((2, span, HD_A), BF),
            pltpu.VMEM((heads, DK, DV), BF),
            pltpu.VMEM((heads, DK, DV), BF),
            pltpu.VMEM((heads, length, DV), F32),
            pltpu.VMEM((heads, length, DK), BF),
            pltpu.VMEM((heads, DK, DK), BF),
            pltpu.VMEM((heads, DK, DV), F32),
            pltpu.VMEM((q_gdn.shape[1] // DK, length, DK), BF),
            pltpu.VMEM((q_gdn.shape[1] // DK, DK, length), BF),
            pltpu.VMEM((heads, length, length), F32),
            pltpu.VMEM((heads, length, DV + DK), BF),
            pltpu.SemaphoreType.DMA((seen,)),
            pltpu.SemaphoreType.DMA((seen,)),
            pltpu.SemaphoreType.DMA((seen,)),
            pltpu.SemaphoreType.DMA((seen,)),
            pltpu.SemaphoreType.DMA((heads,)),
            pltpu.SemaphoreType.DMA((heads,)),
        ],
        compiler_params=pltpu.CompilerParams(collective_id=0, has_side_effects=True),
    )(
        doc_start.reshape(1, length),
        q_gdn,
        k_gdn,
        v_gdn,
        z_gdn,
        beta_logit,
        log_decay,
        norm_weight.reshape(1, DV),
        q_attn,
        k_attn,
        v_attn,
        gate_attn,
    )

    anywhere = pl.BlockSpec(memory_space=pl.ANY)
    return pl.pallas_call(
        store,
        out_shape=(
            jax.ShapeDtypeStruct(v_gdn.shape, BF),
            jax.ShapeDtypeStruct(q_attn.shape, BF),
        ),
        in_specs=[whole] * 2,
        out_specs=(anywhere, anywhere),
        scratch_shapes=[pltpu.SemaphoreType.DMA((2,))],
    )(*[pltpu.with_memory_space_constraint(array, pltpu.VMEM) for array in mixed])


def solution(mesh):
    return jax.shard_map(
        functools.partial(shards, mesh.shape["seq"]),
        mesh=mesh,
        in_specs=(
            P(("groups", "seq")),
            P(("groups", "seq"), "head"),
            P(("groups", "seq"), "head"),
            P(("groups", "seq"), "head"),
            P(("groups", "seq"), "head"),
            P("head", ("groups", "seq")),
            P("head", ("groups", "seq")),
            P(),
            P(("groups", "seq"), "head"),
            P(("groups", "seq"), None),
            P(("groups", "seq"), None),
            P(("groups", "seq"), "head"),
        ),
        out_specs=(P(("groups", "seq"), "head"), P(("groups", "seq"), "head")),
        check_vma=False,
    )
```

```python
import functools

import jax
import jax.numpy as jnp
from jax import lax
from jax.experimental import pallas as pl
from jax.experimental.pallas import tpu as pltpu
from jax.sharding import PartitionSpec as P

DK = 128
DV = 128
QH = 16
KVH = 2
HD_A = 256
NEG = -1e30

MESH = pl.DeviceIdType.MESH
BF = jnp.bfloat16
F32 = jnp.float32


def dot(a, b):
    return jnp.dot(a.astype(BF), b.astype(BF), preferred_element_type=F32)


def dot_t(a, b):
    return lax.dot_general(a, b, (((1,), (1,)), ((), ())), preferred_element_type=F32)


def running_sum(rows, lane):
    width = rows.shape[1]
    step = 1
    while step < width:
        rows = rows + jnp.where(lane >= step, pltpu.roll(rows, step, 1), 0.0)
        step *= 2
    return rows


def kernel(
    devices,
    seen,
    doc_ref,
    q_ref,
    k_ref,
    v_ref,
    z_ref,
    beta_ref,
    gate_ref,
    norm_ref,
    qa_ref,
    ka_ref,
    va_ref,
    ga_ref,
    gdn_ref,
    attn_ref,
    kv_buf,
    state_in,
    state_out,
    local_buf,
    reach_buf,
    map_buf,
    add_buf,
    kn_buf,
    knt_buf,
    decay_buf,
    solved_buf,
    kv_send,
    kv_recv,
    ex_send,
    ex_recv,
    st_send,
    st_recv,
):
    me = lax.axis_index("seq")
    length = q_ref.shape[0]
    heads = v_ref.shape[1] // DV
    key_heads = q_ref.shape[1] // DK
    repeat = heads // key_heads
    attn_heads = qa_ref.shape[1] // HD_A
    kv = lax.axis_index("head") * attn_heads // (QH // KVH)
    columns = pl.ds(pl.multiple_of(kv * HD_A, HD_A), HD_A)
    anchor = me * length

    head = lax.axis_index("head")
    part = head % 2
    partner = head + 1 - 2 * part

    barrier = pltpu.get_barrier_semaphore()
    pl.semaphore_signal(barrier, inc=1, device_id={"head": partner}, device_id_type=MESH)

    @pl.when(me < devices - 1)
    def _():
        pl.semaphore_signal(barrier, inc=1, device_id={"seq": me + 1}, device_id_type=MESH)

    @pl.when(me > 0)
    def _():
        pl.semaphore_signal(barrier, inc=1, device_id={"seq": me - 1}, device_id_type=MESH)

    pl.semaphore_wait(barrier, 1 + jnp.minimum(me, 1) + jnp.minimum(devices - 1 - me, 1))

    def rows_of(r):
        return pl.ds((seen - r) * length, length)

    def hop(r, source):
        return pltpu.make_async_remote_copy(
            src_ref=source,
            dst_ref=kv_buf.at[part, rows_of(r), :],
            send_sem=kv_send.at[r - 1],
            recv_sem=kv_recv.at[r - 1],
            device_id={"seq": me + 1},
            device_id_type=MESH,
        )

    def exchange(r):
        return pltpu.make_async_remote_copy(
            src_ref=kv_buf.at[part, rows_of(r), :],
            dst_ref=kv_buf.at[part, rows_of(r), :],
            send_sem=ex_send.at[r - 1],
            recv_sem=ex_recv.at[r - 1],
            device_id={"head": partner},
            device_id_type=MESH,
        )

    def held(r):
        return kv_buf.at[part, rows_of(r), :]

    def forward(r):
        @pl.when(me >= r)
        def _():
            hop(r, held(r)).wait_recv()
            exchange(r).start()
            if r < seen:
                @pl.when(me < devices - 1)
                def _():
                    hop(r + 1, held(r)).start()

    def state_copy(h):
        return pltpu.make_async_remote_copy(
            src_ref=state_out.at[h],
            dst_ref=state_in.at[h],
            send_sem=st_send.at[h],
            recv_sem=st_recv.at[h],
            device_id={"seq": me + 1},
            device_id_type=MESH,
        )

    @pl.when(me < devices - 1)
    def _():
        for which, source in enumerate((ka_ref, va_ref)):
            @pl.when(part == which)
            def _():
                hop(1, source.at[:, columns]).start()

    row = lax.broadcasted_iota(jnp.int32, (length, length), 0)
    col = lax.broadcasted_iota(jnp.int32, (length, length), 1)
    lane = lax.broadcasted_iota(jnp.int32, (heads, length), 1)
    docs = doc_ref[...]
    run = running_sum(gate_ref[...], lane)
    beta = jax.nn.sigmoid(beta_ref[...])
    alive = docs < anchor
    entry = jnp.where(alive, jnp.exp(run), 0.0)
    last_run = run[:, length - 1 :]
    doc_last = docs[:, length - 1 :]
    tail = jnp.where(doc_last <= anchor + lane, jnp.exp(last_run - run), 0.0)
    entry_last = entry[:, length - 1 :]
    doc_rows = jnp.broadcast_to((docs - anchor).astype(F32), (heads, length))
    stacked = jnp.concatenate([run, beta, entry, doc_rows], axis=0)
    stacked = jnp.concatenate(
        [stacked, jnp.zeros((length - stacked.shape[0], length), F32)], axis=0
    )
    cols = stacked.T

    def column(kind, h):
        at = kind * heads + h
        return cols[:, at : at + 1]

    doc_col = column(3, 0).astype(jnp.int32)
    same = (col <= row) & (doc_col <= col)
    strict = same & (col < row)
    eye = jnp.where(row == col, 1.0, 0.0).astype(F32)
    differ = row ^ col
    levels = 0
    while (1 << levels) < length:
        levels += 1

    ones = jnp.ones((DK, DK), BF)

    def square_sum(values):
        squares = values * values
        high = squares.astype(BF)
        low = (squares - high.astype(F32)).astype(BF)
        return jnp.dot(high, ones, preferred_element_type=F32) + jnp.dot(
            low, ones, preferred_element_type=F32
        )

    def unit_rows(values):
        return values * lax.rsqrt(square_sum(values) + 1e-06)

    gram, knt, lower = {}, {}, {}

    def key_part(g):
        kn = unit_rows(k_ref[:, g * DK : (g + 1) * DK].astype(F32)).astype(BF)
        knt[g] = kn.T
        kn_buf[g] = kn
        knt_buf[g] = knt[g]
        gram[g] = dot(kn, knt[g])

    def gate_part(h):
        spread = jnp.where(same, column(0, h) - run[h : h + 1, :], 0.0)
        decay = jnp.where(same, jnp.exp(spread), 0.0)
        decay_buf[h] = decay
        lower[h] = jnp.where(strict, column(1, h) * decay * gram[h // repeat], 0.0)

    def preparations(group):
        todo = []
        for h in group:
            if h // repeat not in gram:
                gram[h // repeat] = None
                todo.append(functools.partial(key_part, h // repeat))
            todo.append(functools.partial(gate_part, h))
        return todo

    def state_part(group, beside):
        beside = list(beside)
        inverse = {h: eye + lower[h] for h in group}
        for level in range(levels):
            mask = (differ >> level) == 1
            for h in group:
                whole = inverse[h]
                part = jnp.where(mask, whole, 0.0)
                inverse[h] = jnp.where(mask, 0.0, whole) - dot(part, whole)
            if beside:
                beside.pop(0)()
        for task in beside:
            task()
        for h in group:
            g = h // repeat
            values = v_ref[:, h * DV : (h + 1) * DV].astype(F32)
            b = column(1, h)
            right = jnp.concatenate(
                [b * values, (b * column(2, h)) * kn_buf[g].astype(F32)], axis=1
            )
            solved = dot(inverse[h], right).astype(BF)
            solved_buf[h] = solved
            tail_keys = (knt_buf[g].astype(F32) * tail[h : h + 1, :]).astype(BF)
            made = dot(tail_keys, solved)
            map_buf[h] = (entry_last[h : h + 1, :] * eye - made[:, DV:]).astype(BF)
            add_buf[h] = made[:, :DV]
            state_out[h] = made[:, :DV].astype(BF)

        if devices > 1:
            @pl.when(me == 0)
            def _():
                for h in group:
                    state_copy(h).start()

    per_group = 4
    groups = [
        list(range(first, min(first + per_group, heads))) for first in range(0, heads, per_group)
    ]
    for task in preparations(groups[0]):
        task()
    ahead = 0
    for at, group in enumerate(groups):
        state_part(group, preparations(groups[at + 1]) if at + 1 < len(groups) else ())
        if ahead < seen:
            ahead += 1
            forward(ahead)

    def relay(chosen):
        for h in chosen:
            state_copy(h).wait_recv()

            @pl.when(me < devices - 1)
            def _():
                fresh = add_buf[h] + dot(map_buf[h], state_in[h])
                state_out[h] = fresh.astype(BF)
                state_copy(h).start()

    @pl.when(me == 0)
    def _():
        state_in[...] = jnp.zeros(state_in.shape, BF)

    @pl.when(me == 1)
    def _():
        relay(range(heads))

    own = pl.ds(seen * length, length)
    kv_buf[0, own, :] = ka_ref[:, columns]
    kv_buf[1, own, :] = va_ref[:, columns]
    for g in range(key_heads):
        qn = unit_rows(q_ref[:, g * DK : (g + 1) * DK].astype(F32)).astype(BF)
        cross = dot(qn, knt_buf[g])
        for h in range(g * repeat, (g + 1) * repeat):
            made = dot(cross * decay_buf[h], solved_buf[h])
            local_buf[h] = made[:, :DV]
            reach_buf[h] = (column(2, h) * qn.astype(F32) - made[:, DV:]).astype(BF)

    if devices > 2:
        @pl.when(me == 2)
        def _():
            relay(range(heads))

    for r in range(ahead + 1, seen + 1):
        forward(r)
    for r in range(1, seen + 1):
        @pl.when(me >= r)
        def _():
            exchange(r).wait_recv()

        @pl.when(me < r)
        def _():
            kv_buf[:, rows_of(r), :] = jnp.zeros((2, length, HD_A), BF)

    span = (seen + 1) * length
    window = (devices // 2 + 1) * length
    q_at = lax.broadcasted_iota(jnp.int32, (length, span), 0)
    k_at = lax.broadcasted_iota(jnp.int32, (length, span), 1) - seen * length
    floor = jnp.maximum(doc_col, q_at - window + 1)
    visible = (k_at >= floor) & (k_at <= q_at)
    factor = HD_A ** (-0.5)
    for a in range(attn_heads):
        at = slice(a * HD_A, (a + 1) * HD_A)
        raw = dot_t(qa_ref[:, at], kv_buf[0]) * factor
        masked = jnp.where(visible, raw, NEG)
        peak = jnp.max(masked, axis=-1, keepdims=True)
        weights = jnp.exp(masked - peak)
        total = jnp.sum(weights, axis=-1, keepdims=True)
        mixed = jnp.dot(weights.astype(BF), kv_buf[1], preferred_element_type=F32)
        gated = mixed / total * jax.nn.sigmoid(ga_ref[:, at].astype(F32))
        attn_ref[:, at] = gated.astype(BF)

    gain = norm_ref[...]
    pair = 2
    for first in range(0, heads, pair):
        chosen = range(first, min(first + pair, heads))
        if devices > 3:
            @pl.when(me >= 3)
            def _():
                relay(chosen)

        for h in chosen:
            at = slice(h * DV, (h + 1) * DV)
            mixed = local_buf[h] + dot(reach_buf[h], state_in[h])
            spread = lax.rsqrt(square_sum(mixed) * (1.0 / DV) + 1e-06)
            gate = z_ref[:, at].astype(F32)
            gdn_ref[:, at] = (mixed * spread * gain * jax.nn.silu(gate)).astype(BF)

    @pl.when(me < devices - 1)
    def _():
        hop(1, held(1)).wait_send()

    for r in range(1, seen + 1):
        @pl.when(me >= r)
        def _():
            exchange(r).wait_send()
            if r < seen:
                @pl.when(me < devices - 1)
                def _():
                    hop(r + 1, held(r)).wait_send()

    if devices > 1:
        @pl.when(me < devices - 1)
        def _():
            for h in range(heads):
                state_copy(h).wait_send()


def store(first_ref, second_ref, first_out, second_out, sems):
    copies = [
        pltpu.make_async_copy(first_ref, first_out, sems.at[0]),
        pltpu.make_async_copy(second_ref, second_out, sems.at[1]),
    ]
    for copy in copies:
        copy.start()
    for copy in copies:
        copy.wait()


def shards(
    devices,
    doc_start,
    q_gdn,
    k_gdn,
    v_gdn,
    z_gdn,
    beta_logit,
    log_decay,
    norm_weight,
    q_attn,
    k_attn,
    v_attn,
    gate_attn,
):
    length = q_gdn.shape[0]
    heads = v_gdn.shape[1] // DV
    seen = min(devices // 2 + 1, devices - 1)
    span = (seen + 1) * length
    whole = pl.BlockSpec(memory_space=pltpu.VMEM)
    mixed = pl.pallas_call(
        functools.partial(kernel, devices, seen),
        out_shape=(
            pltpu.VMEM(v_gdn.shape, BF),
            pltpu.VMEM(q_attn.shape, BF),
        ),
        in_specs=[whole] * 12,
        out_specs=(whole, whole),
        scratch_shapes=[
            pltpu.VMEM((2, span, HD_A), BF),
            pltpu.VMEM((heads, DK, DV), BF),
            pltpu.VMEM((heads, DK, DV), BF),
            pltpu.VMEM((heads, length, DV), F32),
            pltpu.VMEM((heads, length, DK), BF),
            pltpu.VMEM((heads, DK, DK), BF),
            pltpu.VMEM((heads, DK, DV), F32),
            pltpu.VMEM((q_gdn.shape[1] // DK, length, DK), BF),
            pltpu.VMEM((q_gdn.shape[1] // DK, DK, length), BF),
            pltpu.VMEM((heads, length, length), F32),
            pltpu.VMEM((heads, length, DV + DK), BF),
            pltpu.SemaphoreType.DMA((seen,)),
            pltpu.SemaphoreType.DMA((seen,)),
            pltpu.SemaphoreType.DMA((seen,)),
            pltpu.SemaphoreType.DMA((seen,)),
            pltpu.SemaphoreType.DMA((heads,)),
            pltpu.SemaphoreType.DMA((heads,)),
        ],
        compiler_params=pltpu.CompilerParams(collective_id=0, has_side_effects=True),
    )(
        doc_start.reshape(1, length),
        q_gdn,
        k_gdn,
        v_gdn,
        z_gdn,
        beta_logit,
        log_decay,
        norm_weight.reshape(1, DV),
        q_attn,
        k_attn,
        v_attn,
        gate_attn,
    )

    anywhere = pl.BlockSpec(memory_space=pl.ANY)
    return pl.pallas_call(
        store,
        out_shape=(
            jax.ShapeDtypeStruct(v_gdn.shape, BF),
            jax.ShapeDtypeStruct(q_attn.shape, BF),
        ),
        in_specs=[whole] * 2,
        out_specs=(anywhere, anywhere),
        scratch_shapes=[pltpu.SemaphoreType.DMA((2,))],
    )(*[pltpu.with_memory_space_constraint(array, pltpu.VMEM) for array in mixed])


def solution(mesh):
    return jax.shard_map(
        functools.partial(shards, mesh.shape["seq"]),
        mesh=mesh,
        in_specs=(
            P(("groups", "seq")),
            P(("groups", "seq"), "head"),
            P(("groups", "seq"), "head"),
            P(("groups", "seq"), "head"),
            P(("groups", "seq"), "head"),
            P("head", ("groups", "seq")),
            P("head", ("groups", "seq")),
            P(),
            P(("groups", "seq"), "head"),
            P(("groups", "seq"), None),
            P(("groups", "seq"), None),
            P(("groups", "seq"), "head"),
        ),
        out_specs=(P(("groups", "seq"), "head"), P(("groups", "seq"), "head")),
        check_vma=False,
    )
```
